256 devices in a mesh: lat: 32 (over z, x_lo, core), lon: 8 (over x_hi, y).
Axes of the slice: x: 4 (x_hi: 2, x_lo: 2; x = x_hi * 2 + x_lo), y: 4, z: 8, core: 2. Of those that a mesh axis runs over, the one named last changes fastest.
Arguments:
- cells: bfloat16 [384, 256, 256], P('lat', 'lon'), may hold values from -120 to 120
- w_query: bfloat16 [256, 256], replicated, may hold values from -0.375 to 0.375
- w_key: bfloat16 [256, 256], replicated, may hold values from -0.375 to 0.375
- w_value: bfloat16 [256, 256], replicated, may hold values from -0.375 to 0.375
- w_out: bfloat16 [256, 256], replicated, may hold values from -0.375 to 0.375
- grad_out: bfloat16 [384, 256, 256], P('lat', 'lon'), may hold values from -6 to 6
Outputs:
- mixed: bfloat16 [384, 256, 256], P('lat', 'lon')
- grad_cells: float32 [384, 256, 256], P('lat', 'lon')
- grad_wq: float32 [256, 256], replicated
- grad_wk: float32 [256, 256], replicated
- grad_wv: float32 [256, 256], replicated
- grad_wo: float32 [256, 256], replicated
The draws below stay inside these ranges and needn't reach their ends.
All inputs are finite; a program needn't handle non-finite values.
Results may differ from the reference program's by a relative error of at most 0.004.
The reference program's roundings to bfloat16 on the way count: a program that leaves them out, or rounds other values in their place, can miss the bound.
Values may be sent and summed in bfloat16 or wider, within the bound.
A program may use at most 128 MiB of HBM per device.

```python
import jax
import jax.numpy as jnp
from jax import lax

D = 256
HEADS = 8
REACH = 6
LAT_DEV = 12
LON_DEV = 32
NLAT = 384
NLON = 256


def draw_cells(key, part):
    array_shape = (NLAT, NLON, D)
    ground_key = jax.random.fold_in(key, 0)
    ground = jax.random.normal(ground_key, array_shape, jnp.float32)
    return jnp.clip(ground, -6.0, 6.0).astype(jnp.bfloat16)


def levels(key, extent, cuts, least, largest):
    gain, own = 1.0, jax.random.fold_in(key, 6)
    for dim, shards_of in cuts:
        heights = jnp.exp(jax.random.uniform(jax.random.fold_in(own, dim), (shards_of,), jnp.float32, least / len(cuts), largest / len(cuts)))
        gain = gain * jnp.repeat(heights, extent[dim] // shards_of).reshape([-1 if axis == dim else 1 for axis in range(len(extent))])
    return gain


def normal_values(stream_key, dims, deviation, most, cuts=(), kind=jnp.bfloat16):
    array = jax.random.normal(stream_key, dims, jnp.float32) * deviation
    if len(cuts) > 0:
        array = levels(stream_key, dims, cuts, -0.22, 0.18) * array
    return jnp.clip(array, min=-most, max=most).astype(kind)


def setup_inputs(seed: int = 0) -> dict:
    splits = jax.random.split(jax.random.key(seed), 7)
    return {
        "cells": draw_cells(jax.random.fold_in(splits[6], 71), 0),
        "w_query": normal_values(splits[1], (D, D), D ** -0.5, 0.375),
        "w_key": normal_values(splits[2], (D, D), D ** -0.5, 0.375),
        "w_value": normal_values(splits[3], (D, D), D ** -0.5, 0.375),
        "w_out": normal_values(splits[4], (D, D), D ** -0.5, 0.375),
        "grad_out": normal_values(splits[5], (NLAT, NLON, D), 1.0, 6.0, ((0, 32), (1, 8))),
    }


def window_block(queries, key_vals, grad_heads, valid_rows):
    q_rows, q_cols, model_width = queries.shape
    k_rows, k_cols = key_vals.shape[0], key_vals.shape[1]
    head_dim = model_width // HEADS
    n_query = q_rows * q_cols
    n_key = k_rows * k_cols
    score_scale = head_dim ** -0.5
    row_gap = jnp.arange(k_rows)[None, None, :, None] - jnp.arange(q_rows)[:, None, None, None]
    col_gap = jnp.arange(k_cols)[None, None, None, :] - jnp.arange(q_cols)[None, :, None, None]
    inside = (row_gap >= 0) & (row_gap <= 2 * REACH) & (col_gap >= 0) & (col_gap <= 2 * REACH) & valid_rows[None, None, :, None]
    inside = inside.reshape(n_query, n_key)
    query_heads = queries.reshape(n_query, HEADS, head_dim).astype(jnp.float32)
    key_heads = key_vals[:, :, :model_width].reshape(n_key, HEADS, head_dim).astype(jnp.float32)
    value_heads = key_vals[:, :, model_width:].reshape(n_key, HEADS, head_dim).astype(jnp.float32)
    grad_split = grad_heads.reshape(n_query, HEADS, head_dim).astype(jnp.float32)
    scores = jnp.einsum("qhe,khe->hqk", query_heads, key_heads) * score_scale
    scores = jnp.where(inside[None], scores, -1e30)
    row_max = jnp.max(scores, axis=2, keepdims=True)
    weights = jnp.exp(scores - row_max)
    weights = weights / jnp.sum(weights, axis=2, keepdims=True)
    weights_low = lax.optimization_barrier(weights.astype(jnp.bfloat16)).astype(jnp.float32)
    attended = jnp.einsum("hqk,khe->qhe", weights_low, value_heads).astype(jnp.bfloat16)
    attended = attended.reshape(q_rows, q_cols, model_width)
    grad_weights = jnp.einsum("qhe,khe->hqk", grad_split, value_heads)
    centre = jnp.sum(weights * grad_weights, axis=2, keepdims=True)
    grad_scores = (weights * (grad_weights - centre) * score_scale).astype(jnp.bfloat16)
    grad_scores = lax.optimization_barrier(grad_scores).astype(jnp.float32)
    grad_query = jnp.einsum("hqk,khe->qhe", grad_scores, key_heads).reshape(q_rows, q_cols, model_width)
    grad_key = jnp.einsum("hqk,qhe->khe", grad_scores, query_heads).reshape(k_rows, k_cols, model_width)
    grad_value = jnp.einsum("hqk,qhe->khe", weights_low, grad_split).reshape(k_rows, k_cols, model_width)
    return attended, grad_query, jnp.concatenate([grad_key, grad_value], axis=2)


def back_project(gradient, weight):
    return jnp.dot(gradient.reshape(-1, weight.shape[0]), weight.astype(jnp.float32).T, precision=lax.Precision.HIGHEST)


def reference(cells, w_query, w_key, w_value, w_out, grad_out):
    lat_total, lon_total, model_width = cells.shape
    cells_flat = cells.reshape(-1, model_width)
    queries = jnp.dot(cells_flat, w_query, preferred_element_type=jnp.float32).astype(jnp.bfloat16)
    queries = queries.reshape(lat_total, lon_total, model_width)
    w_pair = jnp.concatenate([w_key, w_value], axis=1)
    key_vals = jnp.dot(cells_flat, w_pair, preferred_element_type=jnp.float32).astype(jnp.bfloat16)
    key_vals = key_vals.reshape(lat_total, lon_total, 2 * model_width)
    grad_heads = jnp.dot(grad_out.reshape(-1, model_width), w_out.T, preferred_element_type=jnp.float32).astype(jnp.bfloat16)
    grad_heads = grad_heads.reshape(lat_total, lon_total, model_width)
    wrapped = jnp.concatenate([key_vals[:, -REACH:], key_vals, key_vals[:, :REACH]], axis=1)
    padded = jnp.pad(wrapped, ((REACH, REACH), (0, 0), (0, 0)))
    lat_index = jnp.arange(lat_total + 2 * REACH) - REACH
    valid_rows = (lat_index >= 0) & (lat_index < lat_total)
    tiles_lat = lat_total // LAT_DEV
    tiles_lon = lon_total // LON_DEV

    def one_tile(grad_pad, tile_index):
        row_start = ((tile_index // tiles_lon) * LAT_DEV).astype(jnp.int32)
        col_start = ((tile_index % tiles_lon) * LON_DEV).astype(jnp.int32)
        anchor = jnp.zeros((), jnp.int32)
        block_q = lax.dynamic_slice(queries, (row_start, col_start, anchor), (LAT_DEV, LON_DEV, model_width))
        ext_shape = (LAT_DEV + 2 * REACH, LON_DEV + 2 * REACH, 2 * model_width)
        block_kv = lax.dynamic_slice(padded, (row_start, col_start, anchor), ext_shape)
        block_grad = lax.dynamic_slice(grad_heads, (row_start, col_start, anchor), (LAT_DEV, LON_DEV, model_width))
        block_valid = lax.dynamic_slice(valid_rows, (row_start,), (LAT_DEV + 2 * REACH,))
        attended, grad_query, grad_kv = window_block(block_q, block_kv, block_grad, block_valid)
        current = lax.dynamic_slice(grad_pad, (row_start, col_start, anchor), ext_shape)
        grad_pad = lax.dynamic_update_slice(grad_pad, current + grad_kv, (row_start, col_start, anchor))
        return grad_pad, (attended, grad_query)

    grad_pad, (attended_tiles, query_tiles) = lax.scan(one_tile, jnp.zeros(padded.shape, jnp.float32), jnp.arange(tiles_lat * tiles_lon, dtype=jnp.int32))

    def assemble(tiles):
        tiles = tiles.reshape(tiles_lat, tiles_lon, LAT_DEV, LON_DEV, model_width)
        return tiles.transpose(0, 2, 1, 3, 4).reshape(lat_total, lon_total, model_width)

    attended = assemble(attended_tiles)
    grad_query = assemble(query_tiles)
    grad_core = grad_pad[REACH:-REACH]
    folded = grad_core[:, REACH:-REACH]
    folded = folded.at[:, :REACH].add(grad_core[:, -REACH:])
    folded = folded.at[:, -REACH:].add(grad_core[:, :REACH])
    grad_key = folded[:, :, :model_width]
    grad_value = folded[:, :, model_width:]
    attended_flat = attended.reshape(-1, model_width)
    mixed = jnp.dot(attended_flat, w_out, preferred_element_type=jnp.float32).astype(jnp.bfloat16)
    mixed = mixed.reshape(lat_total, lon_total, model_width)
    grad_cells = back_project(grad_query, w_query) + back_project(grad_key, w_key) + back_project(grad_value, w_value)
    grad_cells = grad_cells.reshape(lat_total, lon_total, model_width)
    grad_scale = (lat_total * lon_total) ** -0.5
    cells_wide = cells_flat.astype(jnp.float32)
    grad_wq = jnp.dot(cells_wide.T, grad_query.reshape(-1, model_width), precision=lax.Precision.HIGHEST) * grad_scale
    grad_wk = jnp.dot(cells_wide.T, grad_key.reshape(-1, model_width), precision=lax.Precision.HIGHEST) * grad_scale
    grad_wv = jnp.dot(cells_wide.T, grad_value.reshape(-1, model_width), precision=lax.Precision.HIGHEST) * grad_scale
    grad_wo = jnp.dot(attended_flat.T, grad_out.reshape(-1, model_width), preferred_element_type=jnp.float32) * grad_scale
    return mixed, grad_cells, grad_wq, grad_wk, grad_wv, grad_wo
```

```python
import functools

import jax
import jax.numpy as jnp
from jax import lax
from jax.experimental import pallas as pl
from jax.experimental.pallas import tpu as pltpu
from jax.sharding import PartitionSpec as P

HEADS = 8
REACH = 6
EDGE = 8
TILE_ROWS = 4
TILE_COLS = 8
MESH = pl.DeviceIdType.MESH
MOVES = [(a, b) for a in (-1, 0, 1) for b in (-1, 0, 1) if (a, b) != (0, 0)]
BF16 = jnp.bfloat16
F32 = jnp.float32
VMEM_SPEC = pl.BlockSpec(memory_space=pltpu.VMEM)


def nn(a, b):
    return lax.dot_general(a, b, (((1,), (0,)), ((), ())), preferred_element_type=F32)


def nt(a, b):
    return lax.dot_general(a, b, (((1,), (1,)), ((), ())), preferred_element_type=F32)


def tn(a, b):
    return lax.dot_general(a, b, (((0,), (0,)), ((), ())), preferred_element_type=F32)


def split(x):
    high = x.astype(BF16)
    return high, (x - high.astype(F32)).astype(BF16)


def span(move, inner, edge, outer):
    if move == 0:
        return pl.ds(0, inner), pl.ds(outer, inner), pl.ds(outer, inner)
    if move > 0:
        return pl.ds(inner - edge, edge), pl.ds(0, edge), pl.ds(outer + inner, edge)
    return pl.ds(0, edge), pl.ds(outer + inner, edge), pl.ds(0, edge)


def neighbour(a, b):
    n_lat, n_lon = lax.axis_size("lat"), lax.axis_size("lon")
    lat, lon = lax.axis_index("lat"), lax.axis_index("lon")
    return (lax.rem(lat + a + n_lat, n_lat), lax.rem(lon + b + n_lon, n_lon))


def halo_kernel(cells, ext, send, recv, own_sem):
    rows, cols = cells.shape[0], cells.shape[1]
    barrier = pltpu.get_barrier_semaphore()
    for a, b in MOVES:
        pl.semaphore_signal(barrier, inc=1, device_id=neighbour(a, b), device_id_type=MESH)
    own = pltpu.make_async_copy(cells, ext.at[pl.ds(REACH, rows), pl.ds(EDGE, cols)], own_sem)
    own.start()
    pl.semaphore_wait(barrier, len(MOVES))
    copies = []
    for n, (a, b) in enumerate(MOVES):
        row_from, row_to, _ = span(a, rows, REACH, REACH)
        col_from, col_to, _ = span(b, cols, EDGE, EDGE)
        copies.append(
            pltpu.make_async_remote_copy(
                src_ref=cells.at[row_from, col_from],
                dst_ref=ext.at[row_to, col_to],
                send_sem=send.at[n],
                recv_sem=recv.at[n],
                device_id=neighbour(a, b),
                device_id_type=MESH,
            )
        )
        copies[-1].start()
    own.wait()
    for copy in copies:
        copy.wait()


def attend_kernel(
    lat_rows,
    ext,
    cells,
    grad_out,
    wq,
    wk,
    wv,
    wo,
    mixed,
    own_grad,
    ext_grad,
    terms,
    qx,
    gx,
    kx,
    vx,
    ax,
    dqx,
    dkx,
    dvx,
    bias,
    heads_mask,
):
    rows, cols, width = cells.shape
    ext_rows, ext_cols, _ = ext.shape
    n_own, n_ext = rows * cols, ext_rows * ext_cols
    head_dim = width // HEADS
    k_rows, k_cols = TILE_ROWS + 2 * REACH, TILE_COLS + 2 * EDGE
    n_query, n_key = TILE_ROWS * TILE_COLS, k_rows * k_cols
    n_lane = HEADS * n_query
    scale = head_dim ** -0.5
    log2e = 1.4426950408889634

    ext_flat = ext[...].reshape(n_ext, width)
    kx[...] = nn(ext_flat, wk[...]).astype(BF16).astype(F32).reshape(kx.shape)
    vx[...] = nn(ext_flat, wv[...]).astype(BF16).astype(F32).reshape(vx.shape)
    cells_flat = cells[...].reshape(n_own, width)
    out_flat = grad_out[...].reshape(n_own, width)
    qx[...] = nn(cells_flat, wq[...]).astype(BF16).astype(F32).reshape(qx.shape)
    gx[...] = nt(out_flat, wo[...]).astype(BF16).astype(F32).reshape(gx.shape)
    dkx[...] = jnp.zeros_like(dkx)
    dvx[...] = jnp.zeros_like(dvx)

    lane_head = lax.broadcasted_iota(jnp.int32, (n_lane, width), 0) // n_query
    feature_head = lax.broadcasted_iota(jnp.int32, (n_lane, width), 1) // head_dim
    heads_mask[...] = jnp.where(lane_head == feature_head, 1.0, 0.0)

    shape4 = (k_rows, k_cols, n_lane)
    key_row = lax.broadcasted_iota(jnp.int32, shape4, 0)
    key_col = lax.broadcasted_iota(jnp.int32, shape4, 1)
    query = lax.broadcasted_iota(jnp.int32, shape4, 2) % n_query
    row_gap = key_row - query // TILE_COLS
    col_gap = key_col - query % TILE_COLS - (EDGE - REACH)
    inside = (row_gap >= 0) & (row_gap <= 2 * REACH) & (col_gap >= 0) & (col_gap <= 2 * REACH)
    lat_first = lax.axis_index("lat") * rows - REACH
    for i in range(rows // TILE_ROWS):
        lat_row = key_row + (lat_first + i * TILE_ROWS)
        ok = inside & (lat_row >= 0) & (lat_row < lat_rows)
        bias[i] = jnp.where(ok, 0.0, -1e30).reshape(n_key, n_lane)

    col_tiles = cols // TILE_COLS

    def one_tile(t, carry):
        i, j = t // col_tiles, t % col_tiles
        row0 = i * TILE_ROWS
        col0 = pl.multiple_of(j * TILE_COLS, TILE_COLS)
        at_query = (pl.ds(row0, TILE_ROWS), pl.ds(col0, TILE_COLS))
        at_key = (pl.ds(row0, k_rows), pl.ds(col0, k_cols))
        mask = heads_mask[...]
        q_tile = qx[at_query].reshape(n_query, width)
        g_tile = gx[at_query].reshape(n_query, width)
        q_heads = (jnp.concatenate([q_tile] * HEADS, axis=0) * mask).astype(BF16)
        g_heads = (jnp.concatenate([g_tile] * HEADS, axis=0) * mask).astype(BF16)
        k_tile = kx[at_key].reshape(n_key, width).astype(BF16)
        v_tile = vx[at_key].reshape(n_key, width).astype(BF16)
        scores = nt(k_tile, q_heads) * (scale * log2e) + bias[i]
        top = jnp.max(scores, axis=0, keepdims=True)
        weights = jnp.exp2(scores - top)
        weights = weights * (1.0 / jnp.sum(weights, axis=0, keepdims=True))
        low = weights.astype(BF16)
        grad_weights = nt(v_tile, g_heads)
        centre = jnp.sum(weights * grad_weights, axis=0, keepdims=True)
        grad_scores = (weights * (grad_weights - centre) * scale).astype(BF16)
        att = jnp.sum((tn(low, v_tile) * mask).reshape(HEADS, n_query, width), axis=0)
        dq = jnp.sum((tn(grad_scores, k_tile) * mask).reshape(HEADS, n_query, width), axis=0)
        tile_shape = (TILE_ROWS, TILE_COLS, width)
        ax[at_query] = att.astype(BF16).astype(F32).reshape(tile_shape)
        dqx[at_query] = dq.reshape(tile_shape)
        dkx[at_key] += nn(grad_scores, q_heads).reshape(k_rows, k_cols, width)
        dvx[at_key] += nn(low, g_heads).reshape(k_rows, k_cols, width)
        return carry

    lax.fori_loop(0, (rows // TILE_ROWS) * col_tiles, one_tile, 0)

    att = ax[...].reshape(n_own, width).astype(BF16)
    mixed[...] = nn(att, wo[...]).astype(BF16).reshape(mixed.shape)
    terms[pl.ds(3 * width, width)] = tn(att, out_flat)
    q_high, q_low = split(dqx[...].reshape(n_own, width))
    cells_t = cells_flat.T
    terms[pl.ds(0, width)] = nn(cells_t, q_high) + nn(cells_t, q_low)
    own_query = nt(q_high, wq[...]) + nt(q_low, wq[...])
    ext_t = ext_flat.T
    k_high, k_low = split(dkx[...].reshape(n_ext, width))
    v_high, v_low = split(dvx[...].reshape(n_ext, width))
    terms[pl.ds(width, width)] = nn(ext_t, k_high) + nn(ext_t, k_low)
    terms[pl.ds(2 * width, width)] = nn(ext_t, v_high) + nn(ext_t, v_low)
    back = nt(k_high, wk[...]) + nt(k_low, wk[...]) + nt(v_high, wv[...]) + nt(v_low, wv[...])
    kx[...] = back.reshape(kx.shape)
    ext_grad[...] = back.astype(BF16).reshape(ext_grad.shape)
    own_grad[...] = (
        kx[pl.ds(REACH, rows), pl.ds(EDGE, cols), :] + own_query.reshape(own_grad.shape)
    )


def total_kernel(
    chips,
    depth,
    terms,
    ext_grad,
    gathered,
    *refs,
):
    rims = refs[: len(MOVES)]
    (
        pair_in,
        plane_out,
        plane_in,
        column_out,
        column_in,
        result,
        rim_sems,
        pair_sems,
        plane_send,
        plane_recv,
        column_send,
        column_recv,
        spread_send,
        spread_recv,
        relay_send,
        relay_recv,
        self_sem,
    ) = refs[len(MOVES) :]
    lat, lon = lax.axis_index("lat"), lax.axis_index("lon")
    n_lon = lax.axis_size("lon")
    per_plane = chips // n_lon
    core = lat % 2
    x_lo = (lat // 2) % per_plane
    z = lat // (2 * per_plane)
    me = x_lo * n_lon + lon
    partner = (lat + 1 - 2 * core, lon)

    def plane_peer(p):
        return ((z * per_plane + p // n_lon) * 2 + core, p % n_lon)

    def column_peer(w):
        return ((w * per_plane + x_lo) * 2 + core, lon)

    barrier = pltpu.get_barrier_semaphore()

    def greet(device):
        pl.semaphore_signal(barrier, inc=1, device_id=device, device_id_type=MESH)

    greet(partner)
    for step in range(1, chips):
        greet(plane_peer((me + step) % chips))
    for step in range(1, depth):
        greet(column_peer((z + step) % depth))
    for a, b in MOVES:
        greet(neighbour(a, b))
    pl.semaphore_wait(barrier, 1 + (chips - 1) + (depth - 1) + len(MOVES))

    def remote(src, dst, send, recv, device):
        return pltpu.make_async_remote_copy(
            src_ref=src,
            dst_ref=dst,
            send_sem=send,
            recv_sem=recv,
            device_id=device,
            device_id_type=MESH,
        )

    pair = remote(terms.at[1 - core], pair_in, pair_sems.at[0], pair_sems.at[1], partner)
    pair.start()
    rim_copies = []
    rows = ext_grad.shape[0] - 2 * REACH
    cols = ext_grad.shape[1] - 2 * EDGE
    for n, (a, b) in enumerate(MOVES):
        _, _, row_from = span(a, rows, REACH, REACH)
        _, _, col_from = span(b, cols, EDGE, EDGE)
        rim_copies.append(
            remote(
                ext_grad.at[row_from, col_from],
                rims[n],
                rim_sems.at[0, n],
                rim_sems.at[1, n],
                neighbour(a, b),
            )
        )
        rim_copies[-1].start()
    pair.wait()
    plane_out[...] = (terms[core] + pair_in[...]).astype(BF16)
    plane_in[me] = plane_out[me]
    copies = []
    for step in range(1, chips):
        to = (me + step) % chips
        copies.append(
            remote(
                plane_out.at[to],
                plane_in.at[me],
                plane_send.at[step],
                plane_recv.at[step],
                plane_peer(to),
            )
        )
        copies[-1].start()
    for copy in copies:
        copy.wait()
    column_out[...] = jnp.sum(plane_in[...].astype(F32), axis=0)
    column_in[z] = column_out[...]
    copies = []
    for step in range(1, depth):
        to = (z + step) % depth
        copies.append(
            remote(
                column_out,
                column_in.at[z],
                column_send.at[step],
                column_recv.at[step],
                column_peer(to),
            )
        )
        copies[-1].start()
    for copy in copies:
        copy.wait()
    result[...] = jnp.sum(column_in[...], axis=0).astype(BF16)
    copies = []
    own = pltpu.make_async_copy(result, gathered.at[core, me], self_sem)
    own.start()
    for step in range(1, chips):
        to = (me + step) % chips
        copies.append(
            remote(
                result,
                gathered.at[core, me],
                spread_send.at[step],
                spread_recv.at[step],
                plane_peer(to),
            )
        )
        copies[-1].start()
    relays = [
        remote(result, gathered.at[core, me], relay_send.at[0], relay_recv.at[0], partner)
    ]
    relays[0].start()
    for step in range(1, chips):
        copies[step - 1].wait_recv()
        come = (me - step + chips) % chips
        relays.append(
            remote(
                gathered.at[core, come],
                gathered.at[core, come],
                relay_send.at[step],
                relay_recv.at[step],
                partner,
            )
        )
        relays[-1].start()
    own.wait()
    for copy in copies:
        copy.wait_send()
    for relay in relays:
        relay.wait()
    for copy in rim_copies:
        copy.wait()


def finish_kernel(grad_scale, own_grad, gathered, *refs):
    rims = refs[: len(MOVES)]
    grad_cells, *weight_grads = refs[len(MOVES) :]
    rows, cols, width = own_grad.shape
    grad_cells[...] = own_grad[...]
    for n, (a, b) in enumerate(MOVES):
        row_at = (pl.ds(0, rows), pl.ds(0, REACH), pl.ds(rows - REACH, REACH))[a]
        col_at = (pl.ds(0, cols), pl.ds(0, EDGE), pl.ds(cols - EDGE, EDGE))[b]
        grad_cells[row_at, col_at, :] += rims[n][...].astype(F32)
    for n, out in enumerate(weight_grads):
        out[...] = gathered[pl.ds(n * width, width), :].astype(F32) * grad_scale


def call(kernel, outs, count, scratch, **params):
    return pl.pallas_call(
        kernel,
        out_shape=outs,
        in_specs=[VMEM_SPEC] * count,
        out_specs=jax.tree.map(lambda _: VMEM_SPEC, outs),
        scratch_shapes=scratch,
        compiler_params=pltpu.CompilerParams(**params),
    )


def body(cells, w_query, w_key, w_value, w_out, grad_out):
    rows, cols, width = cells.shape
    n_lat, n_lon = lax.axis_size("lat"), lax.axis_size("lon")
    ext_rows, ext_cols = rows + 2 * REACH, cols + 2 * EDGE
    shape = jax.ShapeDtypeStruct
    dma = pltpu.SemaphoreType.DMA

    ext = call(
        halo_kernel,
        shape((ext_rows, ext_cols, width), BF16),
        1,
        [dma((len(MOVES),)), dma((len(MOVES),)), dma],
        collective_id=0,
        has_side_effects=True,
    )(cells)

    own_shape, ext_shape = (rows, cols, width), (ext_rows, ext_cols, width)
    n_query = TILE_ROWS * TILE_COLS
    n_key = (TILE_ROWS + 2 * REACH) * (TILE_COLS + 2 * EDGE)
    mixed, own_grad, ext_grad, terms = call(
        functools.partial(attend_kernel, rows * n_lat),
        (
            shape(own_shape, BF16),
            shape(own_shape, F32),
            shape(ext_shape, BF16),
            shape((4 * width, width), F32),
        ),
        7,
        [pltpu.VMEM(own_shape, F32)] * 2
        + [pltpu.VMEM(ext_shape, F32)] * 2
        + [pltpu.VMEM(own_shape, F32)] * 2
        + [pltpu.VMEM(ext_shape, F32)] * 2
        + [
            pltpu.VMEM((rows // TILE_ROWS, n_key, HEADS * n_query), F32),
            pltpu.VMEM((HEADS * n_query, width), F32),
        ],
        vmem_limit_bytes=60 * 1024 * 1024,
    )(ext, cells, grad_out, w_query, w_key, w_value, w_out)

    chips, depth = 16, n_lat * n_lon // 32
    chunk = 2 * width // chips
    rim_shapes = tuple(
        shape((rows if a == 0 else REACH, cols if b == 0 else EDGE, width), BF16)
        for a, b in MOVES
    )
    gathered, *rims = call(
        functools.partial(total_kernel, chips, depth),
        (shape((2, chips, chunk, width), BF16),) + rim_shapes,
        2,
        [
            pltpu.VMEM((chips, chunk, width), F32),
            pltpu.VMEM((chips, chunk, width), BF16),
            pltpu.VMEM((chips, chunk, width), BF16),
            pltpu.VMEM((chunk, width), F32),
            pltpu.VMEM((depth, chunk, width), F32),
            pltpu.VMEM((chunk, width), BF16),
            dma((2, len(MOVES))),
            dma((2,)),
            dma((chips,)),
            dma((chips,)),
            dma((depth,)),
            dma((depth,)),
            dma((chips,)),
            dma((chips,)),
            dma((chips,)),
            dma((chips,)),
            dma,
        ],
        collective_id=1,
        has_side_effects=True,
    )(terms.reshape(2, chips, chunk, width), ext_grad)

    grad_scale = (rows * n_lat * cols * n_lon) ** -0.5
    grad_cells, grad_wq, grad_wk, grad_wv, grad_wo = call(
        functools.partial(finish_kernel, grad_scale),
        (shape(own_shape, F32),) + (shape((width, width), F32),) * 4,
        2 + len(MOVES),
        [],
    )(own_grad, gathered.reshape(4 * width, width), *rims)
    return mixed, grad_cells, grad_wq, grad_wk, grad_wv, grad_wo


def solution(mesh):
    in_specs = (P("lat", "lon", None), P(), P(), P(), P(), P("lat", "lon", None))
    out_specs = (P("lat", "lon", None), P("lat", "lon", None), P(), P(), P(), P())
    return jax.shard_map(body, mesh=mesh, in_specs=in_specs, out_specs=out_specs, check_vma=False)
```
